32 devices in a mesh: groups: 2 (over x), tile: 16 (over z, y, core).
Axes of the slice: x: 2, y: 2, z: 4, core: 2. Of those that a mesh axis runs over, the one named last changes fastest.
Arguments:
- hidden: bfloat16 [12288, 1152], P(('groups', 'tile')), parts along dimension 0, may hold values from -40 to 40
- keep_mask: int32 [12288], P(('groups', 'tile')), parts along dimension 0, may hold values 0 or 1
- kept_embed: bfloat16 [1152], replicated, may hold values from -6 to 6
- time_mod: bfloat16 [50, 6, 1152], replicated, may hold values from -3 to 3
- timestep: int32 [2], P('groups'), parts along dimension 0, may hold values from 0 to 49
- qkv_weight: bfloat16 [1152, 3456], replicated, may hold values from -0.1875 to 0.1875
- proj_weight: bfloat16 [1152, 1152], replicated, may hold values from -0.1875 to 0.1875
- norm_gain: bfloat16 [1152], replicated, may hold values from 0.099609375 to 1.8984375
- in_weight: bfloat16 [1152, 5760], P('tile'), may hold values from -0.1875 to 0.1875
- in_bias: bfloat16 [5760], replicated, may hold values from -3 to 3
- conv_weight: bfloat16 [3, 3, 5760], replicated, may hold values from -2 to 2
- conv_bias: bfloat16 [5760], replicated, may hold values from -3 to 3
- out_weight: bfloat16 [2880, 1152], P(None, 'tile'), may hold values from -0.109375 to 0.109375
Outputs:
- output: bfloat16 [12288, 1152], P(('groups', 'tile')), parts along dimension 0
The draws below stay inside these ranges and needn't reach their ends.
There are 2 independent parts, one for each index of `groups`. The reference program is written for one: setup_inputs(seed, part) draws one part's arguments, and reference() takes and returns one part's arrays. A program takes and returns all parts, laid end to end along the dimension named above; an argument that names none is the same for every part. Nothing has to cross between parts.
All inputs are finite; a program needn't handle non-finite values. No bound on the sum of `keep_mask` on one device may be relied on, other than what follows from the above.
Results may differ from the reference program's by a relative error of at most 0.0015.
The reference program's roundings to bfloat16 on the way (of `normed_in`, `normed_attn`, `normed_ffn`, `expanded` and `gated`) count: a program that leaves them out, or rounds other values in their place, can miss the bound.
Values may be sent and summed in bfloat16 or wider, within the bound.
A program may use at most 192 MiB of HBM per device.

```python
import math
import jax
import jax.numpy as jnp
from jax import lax

D = 1152
HEADS = 36
HEAD_DIM = 32
FF = 2880
CANVAS_W = 128
NSTEPS = 50
TOKENS = 6144


def draw_hidden(key, part):
    key_base, key_row, key_col = jax.random.split(key, 3)
    row_scale = jnp.exp(jax.random.uniform(key_row, (TOKENS, 1), jnp.float32, math.log(0.4), math.log(4.0)))
    col_scale = jnp.exp(jax.random.uniform(key_col, (1, D), jnp.float32, math.log(0.5), math.log(5.0)))
    base = jnp.clip(jax.random.normal(key_base, (TOKENS, D), jnp.float32), -3.0, 3.0)
    return jnp.clip(base * row_scale * col_scale, -40.0, 40.0).astype(jnp.bfloat16)


def place_ends(values, own_key, smallest, top_value):
    extent = values.shape
    spot = [jax.random.randint(jax.random.fold_in(own_key, axis), (), 0, extent[axis]) for axis in range(len(extent))]
    values = values.at[tuple(spot)].set(smallest)
    longest = extent.index(max(extent))
    spot[longest] = (spot[longest] + 1) % extent[longest]
    return values.at[tuple(spot)].set(top_value)


def levels(key, extent, shards, least, top_value):
    def one(axis_at, blocks):
        steps = jax.random.uniform(jax.random.fold_in(jax.random.fold_in(key, 6), axis_at), (blocks,), jnp.float32, least / len(shards), top_value / len(shards))
        return jnp.repeat(jnp.exp(steps), extent[axis_at] // blocks).reshape((-1,) + (1,) * (len(extent) - axis_at - 1))

    factor_of = one(*shards[0])
    for cut in shards[1:]:
        factor_of = factor_of * one(*cut)
    return factor_of


def scatter_about(own_key, extent, deviation, most, pieces=(), held_as=jnp.bfloat16):
    array = deviation * jax.random.normal(own_key, extent, jnp.float32)
    if pieces:
        array = array * levels(own_key, extent, pieces, -0.22, 0.18)
    return jnp.clip(array, -most, most).astype(held_as)


def setup_inputs(seed: int = 0, part: int = 0) -> dict:
    seeds = jax.random.split(jax.random.key(seed), 14)
    own_keys = jax.random.split(jax.random.fold_in(seeds[13], part), 14)
    hidden = draw_hidden(jax.random.fold_in(jax.random.fold_in(seeds[13], part), 71), part)
    keep_mask = place_ends((jax.random.randint(own_keys[1], (TOKENS,), 0, 2) < 1).astype(jnp.int32), jax.random.fold_in(own_keys[1], 1), 0, 1)
    kept_embed = scatter_about(seeds[2], (D,), 1.0, 6.0)
    time_mod = scatter_about(seeds[3], (NSTEPS, 6, D), 0.5, 3.0)
    timestep = jax.random.randint(own_keys[4], (1,), 0, NSTEPS).astype(jnp.int32)
    qkv_weight = scatter_about(seeds[5], (D, 3 * D), D ** -0.5, 0.1875)
    proj_weight = scatter_about(seeds[6], (D, D), D ** -0.5, 0.1875)
    norm_gain = jnp.clip(1.0 + 0.18 * jax.random.normal(seeds[7], (D,), jnp.float32), 0.099609375, 1.8984375).astype(jnp.bfloat16)
    in_weight = scatter_about(seeds[8], (D, 2 * FF), D ** -0.5, 0.1875, ((0, 16),))
    in_bias = scatter_about(seeds[9], (2 * FF,), 0.5, 3.0)
    conv_weight = scatter_about(seeds[10], (3, 3, 2 * FF), 9 ** -0.5, 2.0)
    conv_bias = scatter_about(seeds[11], (2 * FF,), 0.5, 3.0)
    out_weight = scatter_about(seeds[12], (FF, D), FF ** -0.5, 0.109375, ((1, 16),))
    return dict(hidden=hidden, keep_mask=keep_mask, kept_embed=kept_embed, time_mod=time_mod, timestep=timestep, qkv_weight=qkv_weight, proj_weight=proj_weight, norm_gain=norm_gain, in_weight=in_weight, in_bias=in_bias, conv_weight=conv_weight, conv_bias=conv_bias, out_weight=out_weight)


def modulated_norm(stream, shift, scale):
    factor = lax.rsqrt(lax.optimization_barrier(jnp.mean(stream * stream, axis=-1, keepdims=True)) + 1e-06)
    return stream * factor * (1.0 + scale) + shift

def convolve(window, conv_weight, conv_bias, count):
    width = window.shape[1] - 2
    total = jnp.zeros((count, width, window.shape[2]), jnp.float32) + conv_bias.astype(jnp.float32)
    for row_off in range(3):
        for col_off in range(3):
            total = total + window[row_off:row_off + count, col_off:col_off + width, :].astype(jnp.float32) * conv_weight[row_off, col_off].astype(jnp.float32)
    return total

def reference(hidden, keep_mask, kept_embed, time_mod, timestep, qkv_weight, proj_weight, norm_gain, in_weight, in_bias, conv_weight, conv_bias, out_weight):
    modulation = lax.dynamic_index_in_dim(time_mod, timestep[0], 0, keepdims=False).astype(jnp.float32)
    height = TOKENS // CANVAS_W
    blocks = height // 8
    span = 8 * CANVAS_W
    hidden_blocks = hidden.reshape(blocks, span, D)
    mask_blocks = keep_mask.reshape(blocks, span)
    embed = kept_embed.astype(jnp.float32)

    def residual_in(hidden_rows, mask_rows):
        return hidden_rows.astype(jnp.float32) + mask_rows.astype(jnp.float32)[:, None] * embed[None, :]

    def project(pair):
        stream = residual_in(pair[0], pair[1])
        normed_in = modulated_norm(stream, modulation[0], modulation[1]).astype(jnp.bfloat16)
        mixed_qkv = jnp.dot(normed_in, qkv_weight, preferred_element_type=jnp.float32)
        query = jax.nn.relu(mixed_qkv[:, :D]).astype(jnp.bfloat16)
        key_rows = jax.nn.relu(mixed_qkv[:, D:2 * D]).astype(jnp.bfloat16).reshape(span, HEADS, HEAD_DIM)
        values = mixed_qkv[:, 2 * D:].astype(jnp.bfloat16).reshape(span, HEADS, HEAD_DIM)
        partial_state = jnp.einsum('thd,the->hde', key_rows.astype(jnp.float32), values.astype(jnp.float32), precision=lax.Precision.HIGHEST)
        return (query, partial_state)
    queries, partials = lax.map(project, (hidden_blocks, mask_blocks))
    state = lax.optimization_barrier(jnp.sum(partials, axis=0))

    def attend(triple):
        stream = residual_in(triple[0], triple[1])
        query = triple[2].reshape(span, HEADS, HEAD_DIM).astype(jnp.float32)
        attended = jnp.einsum('thd,hde->the', query, state, precision=lax.Precision.HIGHEST).reshape(span, D)
        factor = lax.rsqrt(lax.optimization_barrier(jnp.mean(attended * attended, axis=-1, keepdims=True)) + 1e-06)
        normed_attn = (attended * factor * norm_gain.astype(jnp.float32)).astype(jnp.bfloat16)
        after_attn = stream + modulation[2] * jnp.dot(normed_attn, proj_weight, preferred_element_type=jnp.float32)
        normed_ffn = modulated_norm(after_attn, modulation[3], modulation[4]).astype(jnp.bfloat16)
        expanded = jax.nn.silu(jnp.dot(normed_ffn, in_weight, preferred_element_type=jnp.float32) + in_bias.astype(jnp.float32)).astype(jnp.bfloat16)
        return (after_attn, expanded)
    residuals, expanded = lax.map(attend, (hidden_blocks, mask_blocks, queries))
    grid = expanded.reshape(height, CANVAS_W, 2 * FF)
    padded = jnp.pad(grid, ((1, 1), (1, 1), (0, 0)))

    def finish(pair):
        first = pair[0] * 8
        window = lax.dynamic_slice_in_dim(padded, first, 10, 0)
        conv = convolve(window, conv_weight, conv_bias, 8)
        gated = (conv[..., :FF] * jax.nn.silu(conv[..., FF:])).astype(jnp.bfloat16).reshape(span, FF)
        return (pair[1] + modulation[5] * jnp.dot(gated, out_weight, preferred_element_type=jnp.float32)).astype(jnp.bfloat16)
    result = lax.map(finish, (jnp.arange(blocks, dtype=jnp.int32), residuals))
    return result.reshape(TOKENS, D)
```

```python
import functools

import jax
import jax.numpy as jnp
from jax import lax
from jax.experimental import pallas as pl
from jax.experimental.pallas import tpu as pltpu
from jax.sharding import PartitionSpec as P

D = 1152
HEADS = 36
HEAD_DIM = 32
FF = 2880
CANVAS_W = 128
LANES = 128
PACK = LANES // HEAD_DIM
GROUPS = D // LANES
MESH = pl.DeviceIdType.MESH


def sum_kernel(n, rows, part_ref, full_ref, landed, mine, send1, recv1, send2, recv2):
    me = lax.axis_index("tile")
    barrier = pltpu.get_barrier_semaphore()

    def greet(k, _):
        pl.semaphore_signal(
            barrier, inc=1, device_id={"tile": lax.rem(me + k, n)}, device_id_type=MESH
        )
        return 0

    lax.fori_loop(1, n, greet, 0)
    pl.semaphore_wait(barrier, n - 1)

    def scatter(k):
        peer = lax.rem(me + k, n)
        return pltpu.make_async_remote_copy(
            src_ref=part_ref.at[peer],
            dst_ref=landed.at[k],
            send_sem=send1.at[k],
            recv_sem=recv1.at[k],
            device_id={"tile": peer},
            device_id_type=MESH,
        )

    def share(k):
        return pltpu.make_async_remote_copy(
            src_ref=mine,
            dst_ref=full_ref.at[me],
            send_sem=send2.at[k],
            recv_sem=recv2.at[k],
            device_id={"tile": lax.rem(me + k, n)},
            device_id_type=MESH,
        )

    def each(do):
        def body(k, _):
            do(k)
            return 0

        lax.fori_loop(1, n, body, 0)

    each(lambda k: scatter(k).start())
    mine[...] = part_ref[me]

    def gather(k):
        scatter(k).wait_recv()
        mine[...] += landed[k]

    each(gather)
    each(lambda k: share(k).start())
    full_ref[me] = mine[...]
    each(lambda k: scatter(k).wait_send())
    each(lambda k: share(k).wait())


def tile_sum(part, n):
    rows = part.shape[1]
    return pl.pallas_call(
        functools.partial(sum_kernel, n, rows),
        out_shape=jax.ShapeDtypeStruct(part.shape, jnp.float32),
        in_specs=[pl.BlockSpec(memory_space=pltpu.VMEM)],
        out_specs=pl.BlockSpec(memory_space=pltpu.VMEM),
        scratch_shapes=[
            pltpu.VMEM((n, rows, LANES), jnp.float32),
            pltpu.VMEM((rows, LANES), jnp.float32),
            pltpu.SemaphoreType.DMA((n,)),
            pltpu.SemaphoreType.DMA((n,)),
            pltpu.SemaphoreType.DMA((n,)),
            pltpu.SemaphoreType.DMA((n,)),
        ],
        compiler_params=pltpu.CompilerParams(collective_id=0, has_side_effects=True),
    )(part)


def modulated_norm(stream, shift, scale):
    factor = lax.rsqrt(jnp.mean(stream * stream, axis=-1, keepdims=True) + 1e-06)
    return stream * factor * (1.0 + scale) + shift


def convolve(window, conv_weight, conv_bias, count):
    width = window.shape[1] - 2
    total = jnp.zeros((count, width, window.shape[2]), jnp.float32) + conv_bias.astype(jnp.float32)
    for row_off in range(3):
        for col_off in range(3):
            total = total + window[row_off : row_off + count, col_off : col_off + width, :].astype(
                jnp.float32
            ) * conv_weight[row_off, col_off].astype(jnp.float32)
    return total


def local(
    n,
    hidden,
    keep_mask,
    kept_embed,
    time_mod,
    timestep,
    qkv_weight,
    proj_weight,
    norm_gain,
    in_weight,
    in_bias,
    conv_weight,
    conv_bias,
    out_weight,
):
    me = lax.axis_index("tile")
    in_full = lax.all_gather(in_weight, "tile", axis=0, tiled=True)
    out_full = lax.all_gather(out_weight, "tile", axis=1, tiled=True)
    modulation = lax.dynamic_index_in_dim(time_mod, timestep[0], 0, keepdims=False).astype(
        jnp.float32
    )
    tokens = hidden.shape[0]
    rows = tokens // CANVAS_W
    stream = (
        hidden.astype(jnp.float32)
        + keep_mask.astype(jnp.float32)[:, None] * kept_embed.astype(jnp.float32)[None, :]
    )
    normed_in = modulated_norm(stream, modulation[0], modulation[1]).astype(jnp.bfloat16)
    mixed_qkv = jnp.dot(normed_in, qkv_weight, preferred_element_type=jnp.float32)
    query = jax.nn.relu(mixed_qkv[:, :D]).astype(jnp.bfloat16)
    key_rows = jax.nn.relu(mixed_qkv[:, D : 2 * D]).astype(jnp.bfloat16)
    values = mixed_qkv[:, 2 * D :].astype(jnp.bfloat16)
    row_head = lax.broadcasted_iota(jnp.int32, (PACK, HEAD_DIM, LANES), 0)
    col_head = lax.broadcasted_iota(jnp.int32, (PACK, HEAD_DIM, LANES), 2) // HEAD_DIM
    same = (row_head == col_head).astype(jnp.float32)
    packed = []
    for g in range(GROUPS):
        cols = slice(g * LANES, (g + 1) * LANES)
        outer = lax.dot_general(
            key_rows[:, cols],
            values[:, cols],
            (((0,), (0,)), ((), ())),
            preferred_element_type=jnp.float32,
        )
        packed.append(jnp.sum(outer.reshape(PACK, HEAD_DIM, LANES) * same, axis=0))
    part = jnp.concatenate(packed, axis=0)
    used = part.shape[0]
    per = -(-used // (8 * n)) * 8
    part = jnp.pad(part, ((0, per * n - used), (0, 0))).reshape(n, per, LANES)
    state = tile_sum(part, n).reshape(n * per, LANES)
    pieces = []
    for g in range(GROUPS):
        block = (state[g * HEAD_DIM : (g + 1) * HEAD_DIM][None] * same).reshape(LANES, LANES)
        pieces.append(
            jnp.dot(
                query[:, g * LANES : (g + 1) * LANES].astype(jnp.float32),
                block,
                precision=lax.Precision.HIGHEST,
            )
        )
    attended = jnp.concatenate(pieces, axis=1)
    factor = lax.rsqrt(jnp.mean(attended * attended, axis=-1, keepdims=True) + 1e-06)
    normed_attn = (attended * factor * norm_gain.astype(jnp.float32)).astype(jnp.bfloat16)
    after_attn = stream + modulation[2] * jnp.dot(
        normed_attn, proj_weight, preferred_element_type=jnp.float32
    )
    normed_ffn = modulated_norm(after_attn, modulation[3], modulation[4]).astype(jnp.bfloat16)
    down = [(i, i + 1) for i in range(n - 1)]
    up = [(i + 1, i) for i in range(n - 1)]
    above = lax.ppermute(normed_ffn[tokens - CANVAS_W :], "tile", down)
    below = lax.ppermute(normed_ffn[:CANVAS_W], "tile", up)
    framed = jnp.concatenate([above, normed_ffn, below], axis=0)
    before = jnp.dot(framed, in_full, preferred_element_type=jnp.float32)
    inner = (
        jax.nn.silu(before + in_bias.astype(jnp.float32))
        .astype(jnp.bfloat16)
        .reshape(rows + 2, CANVAS_W, 2 * FF)
    )
    row_id = lax.broadcasted_iota(jnp.int32, (rows + 2, 1, 1), 0)
    inside = ((row_id > 0) | (me > 0)) & ((row_id < rows + 1) | (me < n - 1))
    inner = jnp.where(inside, inner, jnp.zeros_like(inner))
    padded = jnp.pad(inner, ((0, 0), (1, 1), (0, 0)))
    conv = convolve(padded, conv_weight, conv_bias, rows)
    gated = (conv[..., :FF] * jax.nn.silu(conv[..., FF:])).astype(jnp.bfloat16).reshape(tokens, FF)
    projected = jnp.dot(gated, out_full, preferred_element_type=jnp.float32)
    return (after_attn + modulation[5] * projected).astype(jnp.bfloat16)


def solution(mesh):
    in_specs = (
        P(("groups", "tile"), None),
        P(("groups", "tile")),
        P(),
        P(),
        P("groups"),
        P(),
        P(),
        P(),
        P("tile", None),
        P(),
        P(),
        P(),
        P(None, "tile"),
    )
    return jax.shard_map(
        functools.partial(local, mesh.shape["tile"]),
        mesh=mesh,
        in_specs=in_specs,
        out_specs=P(("groups", "tile"), None),
        check_vma=False,
    )
```

```python
import functools

import jax
import jax.numpy as jnp
from jax import lax
from jax.experimental import pallas as pl
from jax.experimental.pallas import tpu as pltpu
from jax.sharding import PartitionSpec as P

D = 1152
HEADS = 36
HEAD_DIM = 32
FF = 2880
CANVAS_W = 128
LANES = 128
PACK = LANES // HEAD_DIM
GROUPS = D // LANES
MESH = pl.DeviceIdType.MESH


def mesh_box(n):
    wide = 1
    while (2 * wide) ** 2 <= n // 2:
        wide *= 2
    return n // (2 * wide), wide


def front_kernel(
    n,
    hidden_ref,
    mask_ref,
    embed_ref,
    mod_ref,
    qkv_ref,
    proj_ref,
    gain_ref,
    shard_ref,
    full_ref,
    after_ref,
    frame_ref,
    mixed,
    part,
    landed,
    mine,
    state,
    normed,
    send1,
    recv1,
    send2,
    recv2,
    halo_send,
    halo_recv,
    line_send,
    side_send,
    group_send,
    core_send,
    arrive,
    sibling,
    own_sem,
):
    count_a, count_b = mesh_box(n)
    me = lax.axis_index("tile")
    plane = lax.axis_index("groups")
    core = lax.rem(me, 2)
    at_b = lax.rem(me // 2, count_b)
    at_a = me // (2 * count_b)
    rows = shard_ref.shape[0]
    cut = -(-rows // 16) * 8
    rows_of = (slice(0, cut), slice(cut, rows))
    per = mine.shape[0]
    tokens = hidden_ref.shape[0]

    def tile_of(a, b, c):
        return (a * count_b + b) * 2 + c

    barrier = pltpu.get_barrier_semaphore()

    def greet(k, _):
        pl.semaphore_signal(
            barrier, inc=1, device_id={"tile": lax.rem(me + k, n)}, device_id_type=MESH
        )
        return 0

    lax.fori_loop(1, n, greet, 0)
    pl.semaphore_signal(barrier, inc=1, device_id={"groups": 1 - plane}, device_id_type=MESH)
    pl.semaphore_wait(barrier, n)

    def place(a, b, c, p):
        return full_ref.at[tile_of(a, b, c), rows_of[p]]

    def remote(src, a, b, p, send, recv, target):
        return pltpu.make_async_remote_copy(
            src_ref=src,
            dst_ref=place(a, b, core, p),
            send_sem=send,
            recv_sem=recv.at[a, b, p],
            device_id=target,
            device_id_type=MESH,
        )

    def source(a, b, p, own):
        return shard_ref.at[rows_of[p]] if own else place(a, b, core, p)

    def line(a, p, way, own=False):
        return remote(
            source(a, at_b, p, own),
            a,
            at_b,
            p,
            line_send.at[way, a, p],
            arrive,
            {"tile": tile_of(at_a + (1 if way == 0 else -1), at_b, core)},
        )

    def side(a, k, p, own=False):
        return remote(
            source(a, at_b, p, own),
            a,
            at_b,
            p,
            side_send.at[k, a],
            arrive,
            {"tile": tile_of(at_a, lax.rem(at_b + k, count_b), core)},
        )

    def group(a, b, p):
        return remote(
            source(a, b, p, False),
            a,
            b,
            p,
            group_send.at[a, b],
            arrive,
            {"groups": 1 - plane},
        )

    def twin(a, b, p, own=False):
        return remote(
            source(a, b, p, own),
            a,
            b,
            p,
            core_send.at[a, b, p],
            sibling,
            {"tile": tile_of(at_a, at_b, 1 - core)},
        )

    def arrived(a, b, p, recv=arrive, c=None):
        ref = place(a, b, core if c is None else c, p)
        pltpu.make_async_remote_copy(
            src_ref=ref,
            dst_ref=ref,
            send_sem=own_sem,
            recv_sem=recv.at[a, b, p],
            device_id={"tile": tile_of(at_a, at_b, 1 - core)},
            device_id_type=MESH,
        ).wait_recv()

    ways = ((at_a < count_a - 1), (at_a > 0))
    keep = pltpu.make_async_copy(shard_ref, full_ref.at[me], own_sem)
    keep.start()
    for p in range(2):
        for way in range(2):
            @pl.when(ways[way])
            def _():
                line(at_a, p, way, True).start()

        @pl.when(plane == p)
        def _():
            for k in range(1, count_b):
                side(at_a, k, p, True).start()

        twin(at_a, at_b, p, True).start()

    stream = hidden_ref[...].astype(jnp.float32) + mask_ref[...] * embed_ref[...]
    normed[...] = modulated_norm(stream, mod_ref[0:1, :], mod_ref[1:2, :]).astype(jnp.bfloat16)
    after_ref[...] = stream
    span = D // 3

    def project(j, _):
        cols = pl.ds(pl.multiple_of(j * span, LANES), span)
        out = jnp.dot(normed[...], qkv_ref[:, cols], preferred_element_type=jnp.float32)
        out = jnp.where(j < 6, jnp.maximum(out, 0.0), out)
        mixed[:, cols] = out.astype(jnp.bfloat16)
        return 0

    lax.fori_loop(0, 9, project, 0)
    row_head = lax.broadcasted_iota(jnp.int32, (LANES, LANES), 0) // HEAD_DIM
    col_head = lax.broadcasted_iota(jnp.int32, (LANES, LANES), 1) // HEAD_DIM
    same = row_head == col_head
    part[...] = jnp.zeros_like(part)

    def outer(g, _):
        first = pl.multiple_of(g * LANES, LANES)
        product = lax.dot_general(
            mixed[:, pl.ds(D + first, LANES)],
            mixed[:, pl.ds(2 * D + first, LANES)],
            (((0,), (0,)), ((), ())),
            preferred_element_type=jnp.float32,
        )
        product = jnp.where(same, product, 0.0)
        packed = product[:HEAD_DIM]
        for h in range(1, PACK):
            packed = packed + product[h * HEAD_DIM : (h + 1) * HEAD_DIM]
        part[pl.ds(pl.multiple_of(g * HEAD_DIM, HEAD_DIM), HEAD_DIM), :] = packed
        return 0

    lax.fori_loop(0, GROUPS, outer, 0)

    def slot(ref, k):
        return ref.at[pl.ds(pl.multiple_of(k * per, 8), per)]

    def scatter(k):
        peer = lax.rem(me + k, n)
        return pltpu.make_async_remote_copy(
            src_ref=slot(part, peer),
            dst_ref=landed.at[k],
            send_sem=send1.at[k],
            recv_sem=recv1.at[k],
            device_id={"tile": peer},
            device_id_type=MESH,
        )

    def share(k):
        return pltpu.make_async_remote_copy(
            src_ref=mine,
            dst_ref=slot(state, me),
            send_sem=send2.at[k],
            recv_sem=recv2.at[k],
            device_id={"tile": lax.rem(me + k, n)},
            device_id_type=MESH,
        )

    def each(do):
        def body(k, _):
            do(k)
            return 0

        lax.fori_loop(1, n, body, 0)

    each(lambda k: scatter(k).start())
    mine[...] = part[pl.ds(pl.multiple_of(me * per, 8), per), :]

    def gather(k):
        scatter(k).wait_recv()
        mine[...] += landed[k]

    each(gather)
    each(lambda k: share(k).start())
    state[pl.ds(pl.multiple_of(me * per, 8), per), :] = mine[...]
    each(lambda k: scatter(k).wait_send())
    each(lambda k: share(k).wait())

    pieces = []
    for g in range(GROUPS):
        block = jnp.concatenate([state[g * HEAD_DIM : (g + 1) * HEAD_DIM, :]] * PACK, axis=0)
        block = jnp.where(same, block, 0.0)
        pieces.append(
            jnp.dot(
                mixed[:, g * LANES : (g + 1) * LANES].astype(jnp.float32),
                block,
                precision=lax.Precision.HIGHEST,
                preferred_element_type=jnp.float32,
            )
        )
    attended = jnp.concatenate(pieces, axis=1)
    factor = lax.rsqrt(jnp.mean(attended * attended, axis=-1, keepdims=True) + 1e-06)
    normed[...] = (attended * factor * gain_ref[...]).astype(jnp.bfloat16)

    def attach(j, _):
        cols = pl.ds(pl.multiple_of(j * span, LANES), span)
        out = jnp.dot(normed[...], proj_ref[:, cols], preferred_element_type=jnp.float32)
        after_ref[:, cols] += mod_ref[2:3, cols] * out
        return 0

    lax.fori_loop(0, 3, attach, 0)
    frame_ref[CANVAS_W : CANVAS_W + tokens, :] = modulated_norm(
        after_ref[...], mod_ref[3:4, :], mod_ref[4:5, :]
    ).astype(jnp.bfloat16)

    def halo(way):
        lo = tokens if way == 0 else CANVAS_W
        to = 0 if way == 0 else CANVAS_W + tokens
        return pltpu.make_async_remote_copy(
            src_ref=frame_ref.at[lo : lo + CANVAS_W],
            dst_ref=frame_ref.at[to : to + CANVAS_W],
            send_sem=halo_send.at[way],
            recv_sem=halo_recv.at[way],
            device_id={"tile": me + (1 if way == 0 else -1)},
            device_id_type=MESH,
        )

    has = (me < n - 1, me > 0)
    for way in range(2):
        @pl.when(has[way])
        def _():
            halo(way).start()

    @pl.when(me == 0)
    def _():
        frame_ref[:CANVAS_W, :] = jnp.zeros((CANVAS_W, D), jnp.bfloat16)

    @pl.when(me == n - 1)
    def _():
        frame_ref[CANVAS_W + tokens :, :] = jnp.zeros((CANVAS_W, D), jnp.bfloat16)

    def near(d):
        if d == 0:
            return [(at_a, None, 0)]
        return [(at_a - d, at_a >= d, 0), (at_a + d, at_a < count_a - d, 1)]

    def under(cond, do):
        if cond is None:
            do()
        else:
            pl.when(cond)(do)

    for stage in range(1, count_a + 2):
        for a, ok, way in near(stage) if stage < count_a else []:
            def from_line(a=a, way=way):
                for p in range(2):
                    arrived(a, at_b, p)

                    @pl.when(ways[way])
                    def _():
                        line(a, p, way).start()

                    @pl.when(plane == p)
                    def _():
                        for k in range(1, count_b):
                            side(a, k, p).start()

                    twin(a, at_b, p).start()

            under(ok, from_line)
        for a, ok, way in near(stage - 1) if stage - 1 < count_a else []:
            def from_side(a=a):
                for k in range(1, count_b):
                    b = lax.rem(at_b + k, count_b)
                    for p in range(2):
                        @pl.when(plane == p)
                        def _():
                            arrived(a, b, p)
                            group(a, b, p).start()
                            twin(a, b, p).start()

            under(ok, from_side)
        for a, ok, way in near(stage - 2) if 0 <= stage - 2 < count_a else []:
            def from_group(a=a):
                for k in range(1, count_b):
                    b = lax.rem(at_b + k, count_b)
                    for p in range(2):
                        @pl.when(plane != p)
                        def _():
                            arrived(a, b, p)
                            twin(a, b, p).start()

            under(ok, from_group)

    keep.wait()
    for way in range(2):
        @pl.when(has[way])
        def _():
            halo(way).wait_send()

        @pl.when(has[1 - way])
        def _():
            halo(way).wait_recv()

    for a in range(count_a):
        for p in range(2):
            @pl.when(jnp.logical_and(ways[0], at_a >= a))
            def _():
                line(a, p, 0).wait_send()

            @pl.when(jnp.logical_and(ways[1], at_a <= a))
            def _():
                line(a, p, 1).wait_send()

            @pl.when(plane == p)
            def _():
                for k in range(1, count_b):
                    side(a, k, p).wait_send()
                    group(a, lax.rem(at_b + k, count_b), p).wait_send()

            for b in range(count_b):
                twin(a, b, p).wait_send()
                arrived(a, b, p, sibling, 1 - core)


def front(hidden, mask, embed, mod, qkv_weight, proj_weight, gain, shard, n):
    count_a, count_b = mesh_box(n)
    tokens = hidden.shape[0]
    per = -(-GROUPS * HEAD_DIM // (8 * n)) * 8
    vmem = pl.BlockSpec(memory_space=pltpu.VMEM)
    dma = pltpu.SemaphoreType.DMA
    return pl.pallas_call(
        functools.partial(front_kernel, n),
        out_shape=(
            jax.ShapeDtypeStruct((n,) + shard.shape, jnp.bfloat16),
            jax.ShapeDtypeStruct((tokens, D), jnp.float32),
            jax.ShapeDtypeStruct((tokens + 2 * CANVAS_W, D), jnp.bfloat16),
        ),
        in_specs=[vmem] * 7 + [pl.BlockSpec(memory_space=pl.ANY)],
        out_specs=(pl.BlockSpec(memory_space=pl.ANY), vmem, vmem),
        scratch_shapes=[
            pltpu.VMEM((tokens, 3 * D), jnp.bfloat16),
            pltpu.VMEM((n * per, LANES), jnp.float32),
            pltpu.VMEM((n, per, LANES), jnp.float32),
            pltpu.VMEM((per, LANES), jnp.float32),
            pltpu.VMEM((n * per, LANES), jnp.float32),
            pltpu.VMEM((tokens, D), jnp.bfloat16),
            dma((n,)),
            dma((n,)),
            dma((n,)),
            dma((n,)),
            dma((2,)),
            dma((2,)),
            dma((2, count_a, 2)),
            dma((count_b, count_a)),
            dma((count_a, count_b)),
            dma((count_a, count_b, 2)),
            dma((count_a, count_b, 2)),
            dma((count_a, count_b, 2)),
            dma,
        ],
        compiler_params=pltpu.CompilerParams(
            collective_id=0, has_side_effects=True, vmem_limit_bytes=50 << 20
        ),
    )(hidden, mask, embed, mod, qkv_weight, proj_weight, gain, shard)


def modulated_norm(stream, shift, scale):
    factor = lax.rsqrt(jnp.mean(stream * stream, axis=-1, keepdims=True) + 1e-06)
    return stream * factor * (1.0 + scale) + shift


def silu(v):
    half = 0.5 * v
    return half * (1.0 + jnp.tanh(half))


def ffn_kernel(
    edge_ref,
    x_ref,
    wa_ref,
    wb_ref,
    wo_ref,
    pa_ref,
    pb_ref,
    base_ref,
    gate_ref,
    out_ref,
    acc_ref,
):
    step = pl.program_id(0)
    frame = x_ref.shape[0]
    tokens = frame - 2 * CANVAS_W
    x = x_ref[...]
    column = lax.broadcasted_iota(jnp.int32, (CANVAS_W, LANES), 0)
    not_left = column > 0
    not_right = column < CANVAS_W - 1

    def filtered(w_ref, p_ref):
        v = jnp.dot(x, w_ref[...], preferred_element_type=jnp.float32) + p_ref[10:11, :]
        e = silu(v).astype(jnp.bfloat16).astype(jnp.float32)
        lines = [e[r * CANVAS_W : (r + 1) * CANVAS_W] for r in range(frame // CANVAS_W)]
        lines[0] = lines[0] * edge_ref[0]
        lines[-1] = lines[-1] * edge_ref[1]
        out = []
        for r in range(tokens // CANVAS_W):
            side = []
            for j in range(3):
                side.append(
                    lines[r] * p_ref[j : j + 1, :]
                    + lines[r + 1] * p_ref[3 + j : 4 + j, :]
                    + lines[r + 2] * p_ref[6 + j : 7 + j, :]
                )
            left = jnp.where(not_left, pltpu.roll(side[0], 1, 0), 0.0)
            right = jnp.where(not_right, pltpu.roll(side[2], CANVAS_W - 1, 0), 0.0)
            out.append(left + side[1] + right + p_ref[9:10, :])
        return out

    first_half = filtered(wa_ref, pa_ref)
    second_half = filtered(wb_ref, pb_ref)
    gated = jnp.concatenate(
        [(a * silu(b)).astype(jnp.bfloat16) for a, b in zip(first_half, second_half)], axis=0
    )
    part = lax.dot_general(
        gated, wo_ref[...], (((1,), (1,)), ((), ())), preferred_element_type=jnp.float32
    )

    @pl.when(step == 0)
    def _():
        acc_ref[...] = part

    @pl.when(step > 0)
    def _():
        acc_ref[...] += part

    @pl.when(step == pl.num_programs(0) - 1)
    def _():
        out_ref[...] = (base_ref[...] + gate_ref[...] * acc_ref[...]).astype(out_ref.dtype)


def ffn(x, edges, weights, params, base, gate, dtype):
    count = weights.shape[1] // (3 * LANES)
    tokens = base.shape[0]
    whole = lambda shape: pl.BlockSpec(shape, lambda j: (0, 0), pipeline_mode=pl.Buffered(1))
    part = lambda rows, k: pl.BlockSpec((rows, LANES), lambda j, k=k: (0, k * count + j))
    return pl.pallas_call(
        ffn_kernel,
        grid=(count,),
        out_shape=jax.ShapeDtypeStruct(base.shape, dtype),
        in_specs=[
            pl.BlockSpec(memory_space=pltpu.SMEM),
            whole(x.shape),
            part(D, 0),
            part(D, 1),
            part(D, 2),
            part(16, 0),
            part(16, 1),
            whole(base.shape),
            whole(gate.shape),
        ],
        out_specs=pl.BlockSpec(base.shape, lambda j: (0, 0)),
        scratch_shapes=[pltpu.VMEM(base.shape, jnp.float32)],
        compiler_params=pltpu.CompilerParams(vmem_limit_bytes=58 << 20),
        cost_estimate=pl.CostEstimate(
            flops=2 * count * LANES * D * (2 * x.shape[0] + tokens),
            bytes_accessed=2 * weights.size + 8 * base.size,
            transcendentals=0,
        ),
    )(edges, x, weights, weights, weights, params, params, base, gate)


def local(
    n,
    hidden,
    keep_mask,
    kept_embed,
    time_mod,
    timestep,
    qkv_weight,
    proj_weight,
    norm_gain,
    in_weight,
    in_bias,
    conv_weight,
    conv_bias,
    out_weight,
):
    me = lax.axis_index("tile")
    f32 = jnp.float32
    steps = -(-FF // LANES)
    fill = ((0, 0), (0, steps * LANES - FF))
    shard = jnp.concatenate(
        [jnp.pad(piece, fill) for piece in (in_weight[:, :FF], in_weight[:, FF:], out_weight.T)],
        axis=1,
    )
    small = jnp.concatenate(
        [
            conv_weight.reshape(9, 2 * FF).astype(f32),
            conv_bias.astype(f32)[None],
            in_bias.astype(f32)[None],
            jnp.zeros((5, 2 * FF), f32),
        ],
        axis=0,
    )
    table = jnp.concatenate(
        [jnp.pad(small[:, :FF], fill), jnp.pad(small[:, FF:], fill)], axis=1
    )
    modulation = lax.dynamic_index_in_dim(time_mod, timestep[0], 0, keepdims=False).astype(f32)
    full, after_attn, framed = front(
        hidden,
        keep_mask.astype(f32)[:, None],
        kept_embed.astype(f32)[None],
        modulation,
        qkv_weight,
        proj_weight,
        norm_gain.astype(f32)[None],
        shard,
        n,
    )
    edges = jnp.stack([me > 0, me < n - 1]).astype(f32)
    weights = full.reshape(D, shard.shape[1])
    return ffn(framed, edges, weights, table, after_attn, modulation[5][None], jnp.bfloat16)


def solution(mesh):
    in_specs = (
        P(("groups", "tile"), None),
        P(("groups", "tile")),
        P(),
        P(),
        P("groups"),
        P(),
        P(),
        P(),
        P("tile", None),
        P(),
        P(),
        P(),
        P(None, "tile"),
    )
    return jax.shard_map(
        functools.partial(local, mesh.shape["tile"]),
        mesh=mesh,
        in_specs=in_specs,
        out_specs=P(("groups", "tile"), None),
        check_vma=False,
    )
```

```python
import functools

import jax
import jax.numpy as jnp
from jax import lax
from jax.experimental import pallas as pl
from jax.experimental.pallas import tpu as pltpu
from jax.sharding import PartitionSpec as P

D = 1152
HEADS = 36
HEAD_DIM = 32
FF = 2880
CANVAS_W = 128
LANES = 128
PACK = LANES // HEAD_DIM
GROUPS = D // LANES
MESH = pl.DeviceIdType.MESH


def mesh_box(n):
    wide = 1
    while (2 * wide) ** 2 <= n // 2:
        wide *= 2
    return n // (2 * wide), wide


def unit_rows(rows):
    units = 4 if rows >= 32 else 2
    marks = [min(-(-rows * u // (8 * units)) * 8, rows) for u in range(units + 1)]
    return [slice(lo, hi) for lo, hi in zip(marks[:-1], marks[1:])]


def front_kernel(
    n,
    hidden_ref,
    mask_ref,
    embed_ref,
    mod_ref,
    qkv_ref,
    proj_ref,
    gain_ref,
    shard_ref,
    full_ref,
    after_ref,
    frame_ref,
    mixed,
    part,
    landed,
    mine,
    state,
    normed,
    send1,
    recv1,
    send2,
    recv2,
    halo_send,
    halo_recv,
    line_send,
    side_send,
    group_send,
    core_send,
    arrive,
    sibling,
    own_sem,
):
    count_a, count_b = mesh_box(n)
    me = lax.axis_index("tile")
    plane = lax.axis_index("groups")
    core = lax.rem(me, 2)
    at_b = lax.rem(me // 2, count_b)
    at_a = me // (2 * count_b)
    rows = shard_ref.shape[0]
    rows_of = unit_rows(rows)
    units = len(rows_of)
    per = mine.shape[0]
    tokens = hidden_ref.shape[0]

    def tile_of(a, b, c):
        return (a * count_b + b) * 2 + c

    barrier = pltpu.get_barrier_semaphore()

    def greet(k, _):
        pl.semaphore_signal(
            barrier, inc=1, device_id={"tile": lax.rem(me + k, n)}, device_id_type=MESH
        )
        return 0

    lax.fori_loop(1, n, greet, 0)
    pl.semaphore_signal(barrier, inc=1, device_id={"groups": 1 - plane}, device_id_type=MESH)
    pl.semaphore_wait(barrier, n)

    def place(a, b, c, p):
        return full_ref.at[tile_of(a, b, c), rows_of[p]]

    def remote(src, a, b, p, send, recv, target):
        return pltpu.make_async_remote_copy(
            src_ref=src,
            dst_ref=place(a, b, core, p),
            send_sem=send,
            recv_sem=recv.at[a, b, p],
            device_id=target,
            device_id_type=MESH,
        )

    def source(a, b, p, own):
        return shard_ref.at[rows_of[p]] if own else place(a, b, core, p)

    def line(a, p, way, own=False):
        return remote(
            source(a, at_b, p, own),
            a,
            at_b,
            p,
            line_send.at[way, a, p],
            arrive,
            {"tile": tile_of(at_a + (1 if way == 0 else -1), at_b, core)},
        )

    def side(a, k, p, own=False):
        return remote(
            source(a, at_b, p, own),
            a,
            at_b,
            p,
            side_send.at[k, a, p],
            arrive,
            {"tile": tile_of(at_a, lax.rem(at_b + k, count_b), core)},
        )

    def group(a, b, p):
        return remote(
            source(a, b, p, False),
            a,
            b,
            p,
            group_send.at[a, b, p],
            arrive,
            {"groups": 1 - plane},
        )

    def twin(a, b, p, own=False):
        return remote(
            source(a, b, p, own),
            a,
            b,
            p,
            core_send.at[a, b, p],
            sibling,
            {"tile": tile_of(at_a, at_b, 1 - core)},
        )

    def arrived(a, b, p, recv=arrive, c=None):
        ref = place(a, b, core if c is None else c, p)
        pltpu.make_async_remote_copy(
            src_ref=ref,
            dst_ref=ref,
            send_sem=own_sem,
            recv_sem=recv.at[a, b, p],
            device_id={"tile": tile_of(at_a, at_b, 1 - core)},
            device_id_type=MESH,
        ).wait_recv()

    ways = ((at_a < count_a - 1), (at_a > 0))

    def onward(d, p, way):
        if d < count_a - 2:
            return ways[way]
        return jnp.logical_and(ways[way], plane == p % 2)
    keep = pltpu.make_async_copy(shard_ref, full_ref.at[me], own_sem)
    keep.start()
    for p in range(units):
        for way in range(2):
            @pl.when(onward(0, p, way))
            def _():
                line(at_a, p, way, True).start()

        @pl.when(plane == p % 2)
        def _():
            for k in range(1, count_b):
                side(at_a, k, p, True).start()

        twin(at_a, at_b, p, True).start()

    def near(d):
        if d == 0:
            return [(at_a, None, 0)]
        if not 0 < d < count_a:
            return []
        return [(at_a - d, at_a >= d, 0), (at_a + d, at_a < count_a - d, 1)]

    def under(cond, do):
        if cond is None:
            do()
        else:
            pl.when(cond)(do)

    def forward(stage):
        for a, ok, way in near(stage):
            def from_line(a=a, way=way):
                for p in range(units):
                    def one(p=p):
                        arrived(a, at_b, p)
                        if stage < count_a - 1:
                            @pl.when(onward(stage, p, way))
                            def _():
                                line(a, p, way).start()

                        @pl.when(plane == p % 2)
                        def _():
                            for k in range(1, count_b):
                                side(a, k, p).start()
                            if stage == count_a - 1:
                                group(a, at_b, p).start()

                        twin(a, at_b, p).start()

                    under((plane == p % 2) if stage == count_a - 1 else None, one)

            under(ok, from_line)
        for a, ok, way in near(stage - 1):
            def from_side(a=a):
                for p in range(units):
                    if stage - 1 == count_a - 1:
                        @pl.when(plane != p % 2)
                        def _():
                            arrived(a, at_b, p)
                            twin(a, at_b, p).start()

                    @pl.when(plane == p % 2)
                    def _():
                        for k in range(1, count_b):
                            b = lax.rem(at_b + k, count_b)
                            arrived(a, b, p)
                            group(a, b, p).start()
                            twin(a, b, p).start()

            under(ok, from_side)
        for a, ok, way in near(stage - 2):
            def from_group(a=a):
                for p in range(units):
                    @pl.when(plane != p % 2)
                    def _():
                        for k in range(1, count_b):
                            b = lax.rem(at_b + k, count_b)
                            arrived(a, b, p)
                            twin(a, b, p).start()

            under(ok, from_group)

    stream = hidden_ref[...].astype(jnp.float32) + mask_ref[...] * embed_ref[...]
    normed[...] = modulated_norm(stream, mod_ref[0:1, :], mod_ref[1:2, :]).astype(jnp.bfloat16)
    after_ref[...] = stream
    span = D // 3

    def project(j, _):
        cols = pl.ds(pl.multiple_of(j * span, LANES), span)
        out = jnp.dot(normed[...], qkv_ref[:, cols], preferred_element_type=jnp.float32)
        out = jnp.where(j < 6, jnp.maximum(out, 0.0), out)
        mixed[:, cols] = out.astype(jnp.bfloat16)
        return 0

    lax.fori_loop(0, 9, project, 0)
    row_head = lax.broadcasted_iota(jnp.int32, (LANES, LANES), 0) // HEAD_DIM
    col_head = lax.broadcasted_iota(jnp.int32, (LANES, LANES), 1) // HEAD_DIM
    same = row_head == col_head
    part[...] = jnp.zeros_like(part)

    def outer(g, _):
        first = pl.multiple_of(g * LANES, LANES)
        product = lax.dot_general(
            mixed[:, pl.ds(D + first, LANES)],
            mixed[:, pl.ds(2 * D + first, LANES)],
            (((0,), (0,)), ((), ())),
            preferred_element_type=jnp.float32,
        )
        product = jnp.where(same, product, 0.0)
        packed = product[:HEAD_DIM]
        for h in range(1, PACK):
            packed = packed + product[h * HEAD_DIM : (h + 1) * HEAD_DIM]
        part[pl.ds(pl.multiple_of(g * HEAD_DIM, HEAD_DIM), HEAD_DIM), :] = packed
        return 0

    lax.fori_loop(0, GROUPS, outer, 0)

    def slot(ref, k):
        return ref.at[pl.ds(pl.multiple_of(k * per, 8), per)]

    def scatter(k):
        peer = lax.rem(me + k, n)
        return pltpu.make_async_remote_copy(
            src_ref=slot(part, peer),
            dst_ref=landed.at[k],
            send_sem=send1.at[k],
            recv_sem=recv1.at[k],
            device_id={"tile": peer},
            device_id_type=MESH,
        )

    def share(k):
        return pltpu.make_async_remote_copy(
            src_ref=mine,
            dst_ref=slot(state, me),
            send_sem=send2.at[k],
            recv_sem=recv2.at[k],
            device_id={"tile": lax.rem(me + k, n)},
            device_id_type=MESH,
        )

    def each(do):
        def body(k, _):
            do(k)
            return 0

        lax.fori_loop(1, n, body, 0)

    each(lambda k: scatter(k).start())
    forward(1)
    mine[...] = part[pl.ds(pl.multiple_of(me * per, 8), per), :]

    def gather(k):
        scatter(k).wait_recv()
        mine[...] += landed[k]

    each(gather)
    each(lambda k: share(k).start())
    state[pl.ds(pl.multiple_of(me * per, 8), per), :] = mine[...]
    each(lambda k: scatter(k).wait_send())
    each(lambda k: share(k).wait())

    pieces = []
    for g in range(GROUPS):
        block = jnp.concatenate([state[g * HEAD_DIM : (g + 1) * HEAD_DIM, :]] * PACK, axis=0)
        block = jnp.where(same, block, 0.0)
        pieces.append(
            jnp.dot(
                mixed[:, g * LANES : (g + 1) * LANES].astype(jnp.float32),
                block,
                precision=lax.Precision.HIGHEST,
                preferred_element_type=jnp.float32,
            )
        )
    attended = jnp.concatenate(pieces, axis=1)
    factor = lax.rsqrt(jnp.mean(attended * attended, axis=-1, keepdims=True) + 1e-06)
    normed[...] = (attended * factor * gain_ref[...]).astype(jnp.bfloat16)

    def attach(j, _):
        cols = pl.ds(pl.multiple_of(j * span, LANES), span)
        out = jnp.dot(normed[...], proj_ref[:, cols], preferred_element_type=jnp.float32)
        after_ref[:, cols] += mod_ref[2:3, cols] * out
        return 0

    lax.fori_loop(0, 3, attach, 0)
    frame_ref[CANVAS_W : CANVAS_W + tokens, :] = modulated_norm(
        after_ref[...], mod_ref[3:4, :], mod_ref[4:5, :]
    ).astype(jnp.bfloat16)

    def halo(way):
        lo = tokens if way == 0 else CANVAS_W
        to = 0 if way == 0 else CANVAS_W + tokens
        return pltpu.make_async_remote_copy(
            src_ref=frame_ref.at[lo : lo + CANVAS_W],
            dst_ref=frame_ref.at[to : to + CANVAS_W],
            send_sem=halo_send.at[way],
            recv_sem=halo_recv.at[way],
            device_id={"tile": me + (1 if way == 0 else -1)},
            device_id_type=MESH,
        )

    has = (me < n - 1, me > 0)
    for way in range(2):
        @pl.when(has[way])
        def _():
            halo(way).start()

    @pl.when(me == 0)
    def _():
        frame_ref[:CANVAS_W, :] = jnp.zeros((CANVAS_W, D), jnp.bfloat16)

    @pl.when(me == n - 1)
    def _():
        frame_ref[CANVAS_W + tokens :, :] = jnp.zeros((CANVAS_W, D), jnp.bfloat16)

    for stage in range(2, count_a + 2):
        forward(stage)

    keep.wait()
    for way in range(2):
        @pl.when(has[way])
        def _():
            halo(way).wait_send()

        @pl.when(has[1 - way])
        def _():
            halo(way).wait_recv()

    for a in range(count_a):
        far = (at_a - a == count_a - 1, a - at_a == count_a - 1)
        for p in range(units):
            for way in range(2):
                reach = (at_a >= a, at_a <= a)[way]
                last = (at_a - a == count_a - 2, a - at_a == count_a - 2)[way]
                sent = jnp.logical_or(jnp.logical_not(last), plane == p % 2)

                @pl.when(jnp.logical_and(jnp.logical_and(ways[way], reach), sent))
                def _():
                    line(a, p, way).wait_send()

            @pl.when(plane == p % 2)
            def _():
                for k in range(1, count_b):
                    side(a, k, p).wait_send()
                    group(a, lax.rem(at_b + k, count_b), p).wait_send()

                @pl.when(jnp.logical_or(far[0], far[1]))
                def _():
                    group(a, at_b, p).wait_send()

            for b in range(count_b):
                twin(a, b, p).wait_send()
                arrived(a, b, p, sibling, 1 - core)


def front(hidden, mask, embed, mod, qkv_weight, proj_weight, gain, shard, n):
    count_a, count_b = mesh_box(n)
    units = len(unit_rows(shard.shape[0]))
    tokens = hidden.shape[0]
    per = -(-GROUPS * HEAD_DIM // (8 * n)) * 8
    vmem = pl.BlockSpec(memory_space=pltpu.VMEM)
    dma = pltpu.SemaphoreType.DMA
    return pl.pallas_call(
        functools.partial(front_kernel, n),
        out_shape=(
            jax.ShapeDtypeStruct((n,) + shard.shape, jnp.bfloat16),
            jax.ShapeDtypeStruct((tokens, D), jnp.float32),
            jax.ShapeDtypeStruct((tokens + 2 * CANVAS_W, D), jnp.bfloat16),
        ),
        in_specs=[vmem] * 7 + [pl.BlockSpec(memory_space=pl.ANY)],
        out_specs=(pl.BlockSpec(memory_space=pl.ANY), vmem, vmem),
        scratch_shapes=[
            pltpu.VMEM((tokens, 3 * D), jnp.bfloat16),
            pltpu.VMEM((n * per, LANES), jnp.float32),
            pltpu.VMEM((n, per, LANES), jnp.float32),
            pltpu.VMEM((per, LANES), jnp.float32),
            pltpu.VMEM((n * per, LANES), jnp.float32),
            pltpu.VMEM((tokens, D), jnp.bfloat16),
            dma((n,)),
            dma((n,)),
            dma((n,)),
            dma((n,)),
            dma((2,)),
            dma((2,)),
            dma((2, count_a, units)),
            dma((count_b, count_a, units)),
            dma((count_a, count_b, units)),
            dma((count_a, count_b, units)),
            dma((count_a, count_b, units)),
            dma((count_a, count_b, units)),
            dma,
        ],
        compiler_params=pltpu.CompilerParams(
            collective_id=0, has_side_effects=True, vmem_limit_bytes=50 << 20
        ),
    )(hidden, mask, embed, mod, qkv_weight, proj_weight, gain, shard)


def modulated_norm(stream, shift, scale):
    factor = lax.rsqrt(jnp.mean(stream * stream, axis=-1, keepdims=True) + 1e-06)
    return stream * factor * (1.0 + scale) + shift


def silu(v):
    half = 0.5 * v
    return half * (1.0 + jnp.tanh(half))


def ffn_kernel(
    edge_ref,
    x_ref,
    wa_ref,
    wb_ref,
    wo_ref,
    pa_ref,
    pb_ref,
    base_ref,
    gate_ref,
    out_ref,
    acc_ref,
):
    step = pl.program_id(0)
    frame = x_ref.shape[0]
    tokens = frame - 2 * CANVAS_W
    x = x_ref[...]
    column = lax.broadcasted_iota(jnp.int32, (CANVAS_W, LANES), 0)
    not_left = column > 0
    not_right = column < CANVAS_W - 1

    def filtered(w_ref, p_ref):
        v = jnp.dot(x, w_ref[...], preferred_element_type=jnp.float32) + p_ref[10:11, :]
        e = silu(v).astype(jnp.bfloat16).astype(jnp.float32)
        lines = [e[r * CANVAS_W : (r + 1) * CANVAS_W] for r in range(frame // CANVAS_W)]
        lines[0] = lines[0] * edge_ref[0]
        lines[-1] = lines[-1] * edge_ref[1]
        out = []
        for r in range(tokens // CANVAS_W):
            side = []
            for j in range(3):
                side.append(
                    lines[r] * p_ref[j : j + 1, :]
                    + lines[r + 1] * p_ref[3 + j : 4 + j, :]
                    + lines[r + 2] * p_ref[6 + j : 7 + j, :]
                )
            left = jnp.where(not_left, pltpu.roll(side[0], 1, 0), 0.0)
            right = jnp.where(not_right, pltpu.roll(side[2], CANVAS_W - 1, 0), 0.0)
            out.append(left + side[1] + right + p_ref[9:10, :])
        return out

    first_half = filtered(wa_ref, pa_ref)
    second_half = filtered(wb_ref, pb_ref)
    gated = jnp.concatenate(
        [(a * silu(b)).astype(jnp.bfloat16) for a, b in zip(first_half, second_half)], axis=0
    )
    part = lax.dot_general(
        gated, wo_ref[...], (((1,), (1,)), ((), ())), preferred_element_type=jnp.float32
    )

    @pl.when(step == 0)
    def _():
        acc_ref[...] = part

    @pl.when(step > 0)
    def _():
        acc_ref[...] += part

    @pl.when(step == pl.num_programs(0) - 1)
    def _():
        out_ref[...] = (base_ref[...] + gate_ref[...] * acc_ref[...]).astype(out_ref.dtype)


def ffn(x, edges, weights, params, base, gate, dtype):
    count = weights.shape[1] // (3 * LANES)
    tokens = base.shape[0]
    whole = lambda shape: pl.BlockSpec(shape, lambda j: (0, 0), pipeline_mode=pl.Buffered(1))
    part = lambda rows, k: pl.BlockSpec((rows, LANES), lambda j, k=k: (0, k * count + j))
    return pl.pallas_call(
        ffn_kernel,
        grid=(count,),
        out_shape=jax.ShapeDtypeStruct(base.shape, dtype),
        in_specs=[
            pl.BlockSpec(memory_space=pltpu.SMEM),
            whole(x.shape),
            part(D, 0),
            part(D, 1),
            part(D, 2),
            part(16, 0),
            part(16, 1),
            whole(base.shape),
            whole(gate.shape),
        ],
        out_specs=pl.BlockSpec(base.shape, lambda j: (0, 0)),
        scratch_shapes=[pltpu.VMEM(base.shape, jnp.float32)],
        compiler_params=pltpu.CompilerParams(vmem_limit_bytes=58 << 20),
        cost_estimate=pl.CostEstimate(
            flops=2 * count * LANES * D * (2 * x.shape[0] + tokens),
            bytes_accessed=2 * weights.size + 8 * base.size,
            transcendentals=0,
        ),
    )(edges, x, weights, weights, weights, params, params, base, gate)


def local(
    n,
    hidden,
    keep_mask,
    kept_embed,
    time_mod,
    timestep,
    qkv_weight,
    proj_weight,
    norm_gain,
    in_weight,
    in_bias,
    conv_weight,
    conv_bias,
    out_weight,
):
    me = lax.axis_index("tile")
    f32 = jnp.float32
    steps = -(-FF // LANES)
    fill = ((0, 0), (0, steps * LANES - FF))
    shard = jnp.concatenate(
        [jnp.pad(piece, fill) for piece in (in_weight[:, :FF], in_weight[:, FF:], out_weight.T)],
        axis=1,
    )
    small = jnp.concatenate(
        [
            conv_weight.reshape(9, 2 * FF).astype(f32),
            conv_bias.astype(f32)[None],
            in_bias.astype(f32)[None],
            jnp.zeros((5, 2 * FF), f32),
        ],
        axis=0,
    )
    table = jnp.concatenate(
        [jnp.pad(small[:, :FF], fill), jnp.pad(small[:, FF:], fill)], axis=1
    )
    modulation = lax.dynamic_index_in_dim(time_mod, timestep[0], 0, keepdims=False).astype(f32)
    full, after_attn, framed = front(
        hidden,
        keep_mask.astype(f32)[:, None],
        kept_embed.astype(f32)[None],
        modulation,
        qkv_weight,
        proj_weight,
        norm_gain.astype(f32)[None],
        shard,
        n,
    )
    edges = jnp.stack([me > 0, me < n - 1]).astype(f32)
    weights = full.reshape(D, shard.shape[1])
    return ffn(framed, edges, weights, table, after_attn, modulation[5][None], jnp.bfloat16)


def solution(mesh):
    in_specs = (
        P(("groups", "tile"), None),
        P(("groups", "tile")),
        P(),
        P(),
        P("groups"),
        P(),
        P(),
        P(),
        P("tile", None),
        P(),
        P(),
        P(),
        P(None, "tile"),
    )
    return jax.shard_map(
        functools.partial(local, mesh.shape["tile"]),
        mesh=mesh,
        in_specs=in_specs,
        out_specs=P(("groups", "tile"), None),
        check_vma=False,
    )
```

```python
import functools

import jax
import jax.numpy as jnp
from jax import lax
from jax.experimental import pallas as pl
from jax.experimental.pallas import tpu as pltpu
from jax.sharding import PartitionSpec as P

D = 1152
HEADS = 36
HEAD_DIM = 32
FF = 2880
CANVAS_W = 128
LANES = 128
PACK = LANES // HEAD_DIM
GROUPS = D // LANES
MESH = pl.DeviceIdType.MESH


def mesh_box(n):
    wide = 1
    while (2 * wide) ** 2 <= n // 2:
        wide *= 2
    return n // (2 * wide), wide


def unit_rows(rows):
    units = 4 if rows >= 32 else 2
    marks = [min(-(-rows * u // (8 * units)) * 8, rows) for u in range(units + 1)]
    return [slice(lo, hi) for lo, hi in zip(marks[:-1], marks[1:])]


def front_kernel(
    n,
    hidden_ref,
    mask_ref,
    embed_ref,
    mod_ref,
    qkv_ref,
    proj_ref,
    gain_ref,
    shard_ref,
    full_ref,
    after_ref,
    frame_ref,
    mixed,
    part,
    landed,
    mine,
    state,
    normed,
    send1,
    recv1,
    send2,
    recv2,
    halo_send,
    halo_recv,
    line_send,
    side_send,
    group_send,
    core_send,
    arrive,
    sibling,
    own_sem,
):
    count_a, count_b = mesh_box(n)
    me = lax.axis_index("tile")
    plane = lax.axis_index("groups")
    core = lax.rem(me, 2)
    at_b = lax.rem(me // 2, count_b)
    at_a = me // (2 * count_b)
    rows = shard_ref.shape[0]
    rows_of = unit_rows(rows)
    units = len(rows_of)
    per = mine.shape[0]
    tokens = hidden_ref.shape[0]

    def tile_of(a, b, c):
        return (a * count_b + b) * 2 + c

    barrier = pltpu.get_barrier_semaphore()

    def greet(k, _):
        pl.semaphore_signal(
            barrier, inc=1, device_id={"tile": lax.rem(me + k, n)}, device_id_type=MESH
        )
        return 0

    lax.fori_loop(1, n, greet, 0)
    pl.semaphore_signal(barrier, inc=1, device_id={"groups": 1 - plane}, device_id_type=MESH)
    pl.semaphore_wait(barrier, n)

    def place(a, b, c, p):
        return full_ref.at[tile_of(a, b, c), rows_of[p]]

    def remote(src, a, b, p, send, recv, target):
        return pltpu.make_async_remote_copy(
            src_ref=src,
            dst_ref=place(a, b, core, p),
            send_sem=send,
            recv_sem=recv.at[a, b, p],
            device_id=target,
            device_id_type=MESH,
        )

    def source(a, b, p, own):
        return shard_ref.at[rows_of[p]] if own else place(a, b, core, p)

    def line(a, p, way, own=False):
        return remote(
            source(a, at_b, p, own),
            a,
            at_b,
            p,
            line_send.at[way, a, p],
            arrive,
            {"tile": tile_of(at_a + (1 if way == 0 else -1), at_b, core)},
        )

    def side(a, k, p, own=False):
        return remote(
            source(a, at_b, p, own),
            a,
            at_b,
            p,
            side_send.at[k, a, p],
            arrive,
            {"tile": tile_of(at_a, lax.rem(at_b + k, count_b), core)},
        )

    def group(a, b, p):
        return remote(
            source(a, b, p, False),
            a,
            b,
            p,
            group_send.at[a, b, p],
            arrive,
            {"groups": 1 - plane},
        )

    def twin(a, b, p, own=False):
        return remote(
            source(a, b, p, own),
            a,
            b,
            p,
            core_send.at[a, b, p],
            sibling,
            {"tile": tile_of(at_a, at_b, 1 - core)},
        )

    def arrived(a, b, p, recv=arrive, c=None):
        ref = place(a, b, core if c is None else c, p)
        pltpu.make_async_remote_copy(
            src_ref=ref,
            dst_ref=ref,
            send_sem=own_sem,
            recv_sem=recv.at[a, b, p],
            device_id={"tile": tile_of(at_a, at_b, 1 - core)},
            device_id_type=MESH,
        ).wait_recv()

    ways = ((at_a < count_a - 1), (at_a > 0))

    def onward(d, p, way):
        if d < count_a - 2:
            return ways[way]
        return jnp.logical_and(ways[way], plane == p % 2)
    keep = pltpu.make_async_copy(shard_ref, full_ref.at[me], own_sem)
    keep.start()
    for p in range(units):
        for way in range(2):
            @pl.when(onward(0, p, way))
            def _():
                line(at_a, p, way, True).start()

        @pl.when(plane == p % 2)
        def _():
            for k in range(1, count_b):
                side(at_a, k, p, True).start()

        twin(at_a, at_b, p, True).start()

    def near(d):
        if d == 0:
            return [(at_a, None, 0)]
        if not 0 < d < count_a:
            return []
        return [(at_a - d, at_a >= d, 0), (at_a + d, at_a < count_a - d, 1)]

    def under(cond, do):
        if cond is None:
            do()
        else:
            pl.when(cond)(do)

    def forward(stage):
        for a, ok, way in near(stage):
            def from_line(a=a, way=way):
                for p in range(units):
                    def one(p=p):
                        arrived(a, at_b, p)
                        if stage < count_a - 1:
                            @pl.when(onward(stage, p, way))
                            def _():
                                line(a, p, way).start()

                        @pl.when(plane == p % 2)
                        def _():
                            for k in range(1, count_b):
                                side(a, k, p).start()
                            if stage == count_a - 1:
                                group(a, at_b, p).start()

                        twin(a, at_b, p).start()

                    under((plane == p % 2) if stage == count_a - 1 else None, one)

            under(ok, from_line)
        for a, ok, way in near(stage - 1):
            def from_side(a=a):
                for p in range(units):
                    if stage - 1 == count_a - 1:
                        @pl.when(plane != p % 2)
                        def _():
                            arrived(a, at_b, p)
                            twin(a, at_b, p).start()

                    @pl.when(plane == p % 2)
                    def _():
                        for k in range(1, count_b):
                            b = lax.rem(at_b + k, count_b)
                            arrived(a, b, p)
                            group(a, b, p).start()
                            twin(a, b, p).start()

            under(ok, from_side)
        for a, ok, way in near(stage - 2):
            def from_group(a=a):
                for p in range(units):
                    @pl.when(plane != p % 2)
                    def _():
                        for k in range(1, count_b):
                            b = lax.rem(at_b + k, count_b)
                            arrived(a, b, p)
                            twin(a, b, p).start()

            under(ok, from_group)

    stream = hidden_ref[...].astype(jnp.float32) + mask_ref[...] * embed_ref[...]
    normed[...] = modulated_norm(stream, mod_ref[0:1, :], mod_ref[1:2, :]).astype(jnp.bfloat16)
    after_ref[...] = stream
    span = D // 3

    def project(j, _):
        cols = pl.ds(pl.multiple_of(j * span, LANES), span)
        out = jnp.dot(normed[...], qkv_ref[:, cols], preferred_element_type=jnp.float32)
        out = jnp.where(j < 6, jnp.maximum(out, 0.0), out)
        mixed[:, cols] = out.astype(jnp.bfloat16)
        return 0

    lax.fori_loop(0, 9, project, 0)
    row_head = lax.broadcasted_iota(jnp.int32, (LANES, LANES), 0) // HEAD_DIM
    col_head = lax.broadcasted_iota(jnp.int32, (LANES, LANES), 1) // HEAD_DIM
    same = row_head == col_head
    part[...] = jnp.zeros_like(part)

    def outer(g, _):
        first = pl.multiple_of(g * LANES, LANES)
        product = lax.dot_general(
            mixed[:, pl.ds(D + first, LANES)],
            mixed[:, pl.ds(2 * D + first, LANES)],
            (((0,), (0,)), ((), ())),
            preferred_element_type=jnp.float32,
        )
        product = jnp.where(same, product, 0.0)
        packed = product[:HEAD_DIM]
        for h in range(1, PACK):
            packed = packed + product[h * HEAD_DIM : (h + 1) * HEAD_DIM]
        part[pl.ds(pl.multiple_of(g * HEAD_DIM, HEAD_DIM), HEAD_DIM), :] = packed
        return 0

    lax.fori_loop(0, GROUPS, outer, 0)

    def slot(ref, k):
        return ref.at[pl.ds(pl.multiple_of(k * per, 8), per)]

    def scatter(k):
        peer = lax.rem(me + k, n)
        return pltpu.make_async_remote_copy(
            src_ref=slot(part, peer),
            dst_ref=landed.at[k],
            send_sem=send1.at[k],
            recv_sem=recv1.at[k],
            device_id={"tile": peer},
            device_id_type=MESH,
        )

    def share(k):
        return pltpu.make_async_remote_copy(
            src_ref=mine,
            dst_ref=slot(state, me),
            send_sem=send2.at[k],
            recv_sem=recv2.at[k],
            device_id={"tile": lax.rem(me + k, n)},
            device_id_type=MESH,
        )

    def each(do):
        def body(k, _):
            do(k)
            return 0

        lax.fori_loop(1, n, body, 0)

    each(lambda k: scatter(k).start())
    forward(1)
    mine[...] = part[pl.ds(pl.multiple_of(me * per, 8), per), :]

    def gather(k):
        scatter(k).wait_recv()
        mine[...] += landed[k]

    each(gather)
    each(lambda k: share(k).start())
    state[pl.ds(pl.multiple_of(me * per, 8), per), :] = mine[...]
    each(lambda k: scatter(k).wait_send())
    each(lambda k: share(k).wait())

    pieces = []
    for g in range(GROUPS):
        block = jnp.concatenate([state[g * HEAD_DIM : (g + 1) * HEAD_DIM, :]] * PACK, axis=0)
        block = jnp.where(same, block, 0.0)
        pieces.append(
            jnp.dot(
                mixed[:, g * LANES : (g + 1) * LANES].astype(jnp.float32),
                block,
                precision=lax.Precision.HIGHEST,
                preferred_element_type=jnp.float32,
            )
        )
    attended = jnp.concatenate(pieces, axis=1)
    factor = lax.rsqrt(jnp.mean(attended * attended, axis=-1, keepdims=True) + 1e-06)
    normed[...] = (attended * factor * gain_ref[...]).astype(jnp.bfloat16)

    def attach(j, _):
        cols = pl.ds(pl.multiple_of(j * span, LANES), span)
        out = jnp.dot(normed[...], proj_ref[:, cols], preferred_element_type=jnp.float32)
        after_ref[:, cols] += mod_ref[2:3, cols] * out
        return 0

    lax.fori_loop(0, 3, attach, 0)
    frame_ref[CANVAS_W : CANVAS_W + tokens, :] = modulated_norm(
        after_ref[...], mod_ref[3:4, :], mod_ref[4:5, :]
    ).astype(jnp.bfloat16)

    def halo(way):
        lo = tokens if way == 0 else CANVAS_W
        to = 0 if way == 0 else CANVAS_W + tokens
        return pltpu.make_async_remote_copy(
            src_ref=frame_ref.at[lo : lo + CANVAS_W],
            dst_ref=frame_ref.at[to : to + CANVAS_W],
            send_sem=halo_send.at[way],
            recv_sem=halo_recv.at[way],
            device_id={"tile": me + (1 if way == 0 else -1)},
            device_id_type=MESH,
        )

    has = (me < n - 1, me > 0)
    for way in range(2):
        @pl.when(has[way])
        def _():
            halo(way).start()

    @pl.when(me == 0)
    def _():
        frame_ref[:CANVAS_W, :] = jnp.zeros((CANVAS_W, D), jnp.bfloat16)

    @pl.when(me == n - 1)
    def _():
        frame_ref[CANVAS_W + tokens :, :] = jnp.zeros((CANVAS_W, D), jnp.bfloat16)

    for stage in range(2, count_a + 2):
        forward(stage)

    keep.wait()
    for way in range(2):
        @pl.when(has[way])
        def _():
            halo(way).wait_send()

        @pl.when(has[1 - way])
        def _():
            halo(way).wait_recv()

    for a in range(count_a):
        far = (at_a - a == count_a - 1, a - at_a == count_a - 1)
        for p in range(units):
            for way in range(2):
                reach = (at_a >= a, at_a <= a)[way]
                last = (at_a - a == count_a - 2, a - at_a == count_a - 2)[way]
                sent = jnp.logical_or(jnp.logical_not(last), plane == p % 2)

                @pl.when(jnp.logical_and(jnp.logical_and(ways[way], reach), sent))
                def _():
                    line(a, p, way).wait_send()

            @pl.when(plane == p % 2)
            def _():
                for k in range(1, count_b):
                    side(a, k, p).wait_send()
                    group(a, lax.rem(at_b + k, count_b), p).wait_send()

                @pl.when(jnp.logical_or(far[0], far[1]))
                def _():
                    group(a, at_b, p).wait_send()

            for b in range(count_b):
                twin(a, b, p).wait_send()
                arrived(a, b, p, sibling, 1 - core)


def front(hidden, mask, embed, mod, qkv_weight, proj_weight, gain, shard, n):
    count_a, count_b = mesh_box(n)
    units = len(unit_rows(shard.shape[0]))
    tokens = hidden.shape[0]
    per = -(-GROUPS * HEAD_DIM // (8 * n)) * 8
    vmem = pl.BlockSpec(memory_space=pltpu.VMEM)
    dma = pltpu.SemaphoreType.DMA
    return pl.pallas_call(
        functools.partial(front_kernel, n),
        out_shape=(
            jax.ShapeDtypeStruct((n,) + shard.shape, jnp.bfloat16),
            jax.ShapeDtypeStruct((tokens, D), jnp.float32),
            jax.ShapeDtypeStruct((tokens + 2 * CANVAS_W, D), jnp.bfloat16),
        ),
        in_specs=[vmem] * 7 + [pl.BlockSpec(memory_space=pl.ANY)],
        out_specs=(pl.BlockSpec(memory_space=pl.ANY), vmem, vmem),
        scratch_shapes=[
            pltpu.VMEM((tokens, 3 * D), jnp.bfloat16),
            pltpu.VMEM((n * per, LANES), jnp.float32),
            pltpu.VMEM((n, per, LANES), jnp.float32),
            pltpu.VMEM((per, LANES), jnp.float32),
            pltpu.VMEM((n * per, LANES), jnp.float32),
            pltpu.VMEM((tokens, D), jnp.bfloat16),
            dma((n,)),
            dma((n,)),
            dma((n,)),
            dma((n,)),
            dma((2,)),
            dma((2,)),
            dma((2, count_a, units)),
            dma((count_b, count_a, units)),
            dma((count_a, count_b, units)),
            dma((count_a, count_b, units)),
            dma((count_a, count_b, units)),
            dma((count_a, count_b, units)),
            dma,
        ],
        compiler_params=pltpu.CompilerParams(
            collective_id=0, has_side_effects=True, vmem_limit_bytes=50 << 20
        ),
    )(hidden, mask, embed, mod, qkv_weight, proj_weight, gain, shard)


def modulated_norm(stream, shift, scale):
    factor = lax.rsqrt(jnp.mean(stream * stream, axis=-1, keepdims=True) + 1e-06)
    return stream * factor * (1.0 + scale) + shift


def silu(v):
    half = 0.5 * v
    return half * (1.0 + jnp.tanh(half))


def ffn_kernel(
    edge_ref,
    x_ref,
    wa_ref,
    wb_ref,
    wo_ref,
    pa_ref,
    pb_ref,
    base_ref,
    gate_ref,
    out_ref,
    acc_ref,
):
    step = pl.program_id(0)
    frame = x_ref.shape[0]
    tokens = frame - 2 * CANVAS_W
    x = x_ref[...]
    column = lax.broadcasted_iota(jnp.int32, (CANVAS_W, LANES), 0)
    not_left = column > 0
    not_right = column < CANVAS_W - 1

    both = jnp.concatenate([wa_ref[...], wb_ref[...]], axis=1)
    wide = jnp.dot(x, both, preferred_element_type=jnp.float32)

    def filtered(v, p_ref):
        e = silu(v + p_ref[10:11, :]).astype(jnp.bfloat16).astype(jnp.float32)
        lines = [e[r * CANVAS_W : (r + 1) * CANVAS_W] for r in range(frame // CANVAS_W)]
        lines[0] = lines[0] * edge_ref[0]
        lines[-1] = lines[-1] * edge_ref[1]
        out = []
        for r in range(tokens // CANVAS_W):
            side = []
            for j in range(3):
                side.append(
                    lines[r] * p_ref[j : j + 1, :]
                    + lines[r + 1] * p_ref[3 + j : 4 + j, :]
                    + lines[r + 2] * p_ref[6 + j : 7 + j, :]
                )
            left = jnp.where(not_left, pltpu.roll(side[0], 1, 0), 0.0)
            right = jnp.where(not_right, pltpu.roll(side[2], CANVAS_W - 1, 0), 0.0)
            out.append(left + side[1] + right + p_ref[9:10, :])
        return out

    first_half = filtered(wide[:, :LANES], pa_ref)
    second_half = filtered(wide[:, LANES:], pb_ref)
    gated = jnp.concatenate(
        [(a * silu(b)).astype(jnp.bfloat16) for a, b in zip(first_half, second_half)], axis=0
    )
    part = lax.dot_general(
        gated, wo_ref[...], (((1,), (1,)), ((), ())), preferred_element_type=jnp.float32
    )

    @pl.when(step == 0)
    def _():
        acc_ref[...] = part

    @pl.when(step > 0)
    def _():
        acc_ref[...] += part

    @pl.when(step == pl.num_programs(0) - 1)
    def _():
        out_ref[...] = (base_ref[...] + gate_ref[...] * acc_ref[...]).astype(out_ref.dtype)


def ffn(x, edges, weights, params, base, gate, dtype):
    count = weights.shape[1] // (3 * LANES)
    tokens = base.shape[0]
    whole = lambda shape: pl.BlockSpec(shape, lambda j: (0, 0), pipeline_mode=pl.Buffered(1))
    part = lambda rows, k: pl.BlockSpec((rows, LANES), lambda j, k=k: (0, k * count + j))
    return pl.pallas_call(
        ffn_kernel,
        grid=(count,),
        out_shape=jax.ShapeDtypeStruct(base.shape, dtype),
        in_specs=[
            pl.BlockSpec(memory_space=pltpu.SMEM),
            whole(x.shape),
            part(D, 0),
            part(D, 1),
            part(D, 2),
            part(16, 0),
            part(16, 1),
            whole(base.shape),
            whole(gate.shape),
        ],
        out_specs=pl.BlockSpec(base.shape, lambda j: (0, 0)),
        scratch_shapes=[pltpu.VMEM(base.shape, jnp.float32)],
        compiler_params=pltpu.CompilerParams(vmem_limit_bytes=58 << 20),
        cost_estimate=pl.CostEstimate(
            flops=2 * count * LANES * D * (2 * x.shape[0] + tokens),
            bytes_accessed=2 * weights.size + 8 * base.size,
            transcendentals=0,
        ),
    )(edges, x, weights, weights, weights, params, params, base, gate)


def local(
    n,
    hidden,
    keep_mask,
    kept_embed,
    time_mod,
    timestep,
    qkv_weight,
    proj_weight,
    norm_gain,
    in_weight,
    in_bias,
    conv_weight,
    conv_bias,
    out_weight,
):
    me = lax.axis_index("tile")
    f32 = jnp.float32
    steps = -(-FF // LANES)
    fill = ((0, 0), (0, steps * LANES - FF))
    shard = jnp.concatenate(
        [jnp.pad(piece, fill) for piece in (in_weight[:, :FF], in_weight[:, FF:], out_weight.T)],
        axis=1,
    )
    small = jnp.concatenate(
        [
            conv_weight.reshape(9, 2 * FF).astype(f32),
            conv_bias.astype(f32)[None],
            in_bias.astype(f32)[None],
            jnp.zeros((5, 2 * FF), f32),
        ],
        axis=0,
    )
    table = jnp.concatenate(
        [jnp.pad(small[:, :FF], fill), jnp.pad(small[:, FF:], fill)], axis=1
    )
    modulation = lax.dynamic_index_in_dim(time_mod, timestep[0], 0, keepdims=False).astype(f32)
    full, after_attn, framed = front(
        hidden,
        keep_mask.astype(f32)[:, None],
        kept_embed.astype(f32)[None],
        modulation,
        qkv_weight,
        proj_weight,
        norm_gain.astype(f32)[None],
        shard,
        n,
    )
    edges = jnp.stack([me > 0, me < n - 1]).astype(f32)
    weights = full.reshape(D, shard.shape[1])
    return ffn(framed, edges, weights, table, after_attn, modulation[5][None], jnp.bfloat16)


def solution(mesh):
    in_specs = (
        P(("groups", "tile"), None),
        P(("groups", "tile")),
        P(),
        P(),
        P("groups"),
        P(),
        P(),
        P(),
        P("tile", None),
        P(),
        P(),
        P(),
        P(None, "tile"),
    )
    return jax.shard_map(
        functools.partial(local, mesh.shape["tile"]),
        mesh=mesh,
        in_specs=in_specs,
        out_specs=P(("groups", "tile"), None),
        check_vma=False,
    )
```
